128 devices in a mesh: phrase: 16 (over y, z_lo, core), vocab: 8 (over x, z_hi).
Axes of the slice: x: 4, y: 4, z: 4 (z_hi: 2, z_lo: 2; z = z_hi * 2 + z_lo), core: 2. Of those that a mesh axis runs over, the one named last changes fastest.
Arguments:
- frames: bfloat16 [1536, 1024], P(('phrase', 'vocab'))
- frame_lens: int32 [4], replicated, may hold values from 192 to 384, as said below
- labels: int32 [4, 64], replicated, may hold values from 1 to 4095
- label_lens: int32 [4], replicated, may hold values from 16 to 63, as said below
- phrase_ids: int32 [65536, 8], P(('phrase', 'vocab')), may hold values from 0 to 4095
- phrase_lens: int32 [65536], P(('phrase', 'vocab')), may hold values from 1 to 8
- phrase_table: bfloat16 [4096, 512], replicated, may hold values from -6 to 6
- phrase_w: bfloat16 [512, 512], replicated, may hold values from -0.25 to 0.25
- key_w: bfloat16 [512, 512], replicated, may hold values from -0.25 to 0.25
- value_w: bfloat16 [512, 512], replicated, may hold values from -0.25 to 0.25
- query_w: bfloat16 [1024, 512], replicated, may hold values from -0.9375 to 0.9375
- context_w: bfloat16 [512, 1024], replicated, may hold values from -0.25 to 0.25
- joint_enc_w: bfloat16 [1024, 640], replicated, may hold values from -0.1875 to 0.1875
- pred_table: bfloat16 [4096, 640], replicated, may hold values from -6 to 6
- pred_w: bfloat16 [640, 640], replicated, may hold values from -0.25 to 0.25
- out_w: bfloat16 [640, 4096], P(None, 'vocab')
Outputs:
- blank_logp: float32 [1536, 64], P('phrase', 'vocab')
- label_logp: float32 [1536, 64], P('phrase', 'vocab')
The draws below stay inside these ranges and needn't reach their ends.
Inputs may be any that keep to these rules, and one draw needn't show every extreme that they name: `frame_lens`: some utterance has exactly 384 frames. `label_lens`: some utterance has exactly 63 labels.
All inputs are finite; a program needn't handle non-finite values.
Results may differ from the reference program's by a relative error of at most 0.0034.
Values may be sent and summed in bfloat16 or wider, within the bound.
No kernel may reach another device: no remote copies, remote signals or barrier semaphores. Data moves between devices by JAX's collectives and lax.ppermute only.
A program may use at most 128 MiB of HBM per device.

```python
import math
import jax
import jax.numpy as jnp
import numpy as np
from jax import lax

D = 1024
E = 512
HEADS = 4
HD = 128
JH = 640
V = 4096
PLEN = 8
UTT = 4
LPOS = 64
FR_DEV = 96
PH_DEV = 512
FRAMES = 1536
TLEN = 384
PHRASES = 65536


def draw_frames(key, part):
    base = jnp.clip(jax.random.normal(key, (FRAMES, D), jnp.float32), -6.0, 6.0)
    return base.astype(jnp.bfloat16)


def draw_frame_lens(key, part):
    lens = jax.random.randint(jax.random.fold_in(key, 1), (UTT,), TLEN // 2, TLEN + 1)
    full = jax.random.randint(jax.random.fold_in(key, 2), (), 0, UTT)
    return jnp.where(jnp.arange(UTT) == full, TLEN, lens).astype(jnp.int32)


def draw_label_lens(key, part):
    lens = jax.random.randint(jax.random.fold_in(key, 3), (UTT,), LPOS // 4, LPOS)
    full = jax.random.randint(jax.random.fold_in(key, 4), (), 0, UTT)
    return jnp.where(jnp.arange(UTT) == full, LPOS - 1, lens).astype(jnp.int32)


def draw_out_w(key, part):
    base = jnp.clip(jax.random.normal(key, (JH, V), jnp.float32), -6.0, 6.0) * (5.0 / math.sqrt(JH))
    return base.astype(jnp.bfloat16)


def set_ends(values, key, smallest, high):
    dims = values.shape
    index_at = [jax.random.randint(jax.random.fold_in(key, axis), (), 0, dims[axis]) for axis in range(len(dims))]
    values = values.at[tuple(index_at)].set(smallest)
    longest = dims.index(max(dims))
    index_at[longest] = (index_at[longest] + 1) % dims[longest]
    return values.at[tuple(index_at)].set(high)


def cumulative_ranks(number_of, slope):
    portions = [(1 << 20) // math.isqrt(standing ** slope) + 1 for standing in range(1, number_of + 1)]
    width = 1 + sum(portions) // (1 << 30)
    return np.cumsum(np.array([max(1, weight // width) for weight in portions]))


def ranked(key, shape, count, lean):
    listing = cumulative_ranks(count, lean)
    lot = jax.random.randint(jax.random.fold_in(key, 1), shape, 0, int(listing[count - 1]))
    rank = jnp.searchsorted(jnp.asarray(listing, jnp.int32), lot, side="right")
    return jax.random.permutation(jax.random.fold_in(key, 2), count)[rank].astype(jnp.int32)


def centred(own_key, shape, spread, reach, held_as=jnp.bfloat16):
    values = jax.random.normal(own_key, shape, jnp.float32) * spread
    return jnp.minimum(jnp.maximum(values, -reach), reach).astype(held_as)


def setup_inputs(seed: int = 0) -> dict:
    splits = jax.random.split(jax.random.key(seed), 17)
    return {
        "frames": draw_frames(jax.random.fold_in(splits[16], 71), 0),
        "frame_lens": draw_frame_lens(jax.random.fold_in(splits[16], 71), 0),
        "labels": set_ends(jax.random.randint(splits[2], (UTT, LPOS), 1, V), jax.random.fold_in(splits[2], 1), 1, V - 1).astype(jnp.int32),
        "label_lens": draw_label_lens(jax.random.fold_in(splits[16], 71), 0),
        "phrase_ids": set_ends(ranked(splits[4], (PHRASES, PLEN), V, 2), jax.random.fold_in(splits[4], 3), 0, V - 1).astype(jnp.int32),
        "phrase_lens": set_ends(jax.random.randint(splits[5], (PHRASES,), 1, PLEN + 1), jax.random.fold_in(splits[5], 1), 1, PLEN).astype(jnp.int32),
        "phrase_table": centred(splits[6], (V, E), 1.0, 6.0),
        "phrase_w": centred(splits[7], (E, E), E ** -0.5, 0.25),
        "key_w": centred(splits[8], (E, E), E ** -0.5, 0.25),
        "value_w": centred(splits[9], (E, E), E ** -0.5, 0.25),
        "query_w": centred(splits[10], (D, E), (5.0 / D ** 0.5), 0.9375),
        "context_w": centred(splits[11], (E, D), E ** -0.5, 0.25),
        "joint_enc_w": centred(splits[12], (D, JH), D ** -0.5, 0.1875),
        "pred_table": centred(splits[13], (V, JH), 1.0, 6.0),
        "pred_w": centred(splits[14], (JH, JH), JH ** -0.5, 0.25),
        "out_w": draw_out_w(jax.random.fold_in(splits[16], 71), 0),
    }


def encode(ids, lens, phrase_table, phrase_w):
    emb = phrase_table[ids].astype(jnp.float32)
    mask = (jnp.arange(ids.shape[1], dtype=jnp.int32)[None, :] < lens[:, None]).astype(jnp.float32)
    summed = jnp.einsum('npe,np->ne', emb, mask)
    mean = (summed / lens[:, None].astype(jnp.float32)).astype(jnp.bfloat16)
    return jnp.tanh(jnp.dot(mean, phrase_w, preferred_element_type=jnp.float32)).astype(jnp.bfloat16)

def reference(frames, frame_lens, labels, label_lens, phrase_ids, phrase_lens, phrase_table, phrase_w, key_w, value_w, query_w, context_w, joint_enc_w, pred_table, pred_w, out_w):
    ids_blocks = phrase_ids.reshape(-1, PH_DEV, PLEN)
    len_blocks = phrase_lens.reshape(-1, PH_DEV)
    phrase_vec = lax.map(lambda pair: encode(pair[0], pair[1], phrase_table, phrase_w), (ids_blocks, len_blocks)).reshape(PHRASES, E)
    keys = jnp.dot(phrase_vec, key_w, preferred_element_type=jnp.float32).astype(jnp.bfloat16)
    values = jnp.dot(phrase_vec, value_w, preferred_element_type=jnp.float32).astype(jnp.bfloat16)
    queries = jnp.dot(frames, query_w, preferred_element_type=jnp.float32).astype(jnp.bfloat16)
    nblocks = PHRASES // PH_DEV
    key_f = keys.astype(jnp.float32).reshape(PHRASES, HEADS, HD)
    value_f = values.astype(jnp.float32).reshape(nblocks, PH_DEV, HEADS, HD)
    scale = 1.0 / math.sqrt(HD)

    def attend(block):
        qf = block.astype(jnp.float32).reshape(-1, HEADS, HD)
        scores = (jnp.einsum('fhd,phd->fhp', qf, key_f) * scale).reshape(qf.shape[0], HEADS, nblocks, PH_DEV)
        block_peak = lax.optimization_barrier(jnp.max(scores, -1))
        weights = jnp.exp(scores - block_peak[..., None]).astype(jnp.bfloat16)
        wf = weights.astype(jnp.float32)
        block_total = lax.optimization_barrier(jnp.sum(wf, -1))
        block_numer = jnp.einsum('fhbp,bphd->fhbd', wf, value_f)
        peak = lax.optimization_barrier(jnp.max(block_peak, -1))
        factor = jnp.exp(block_peak - peak[..., None])
        total = lax.optimization_barrier(jnp.sum(block_total * factor, -1))
        numer = lax.optimization_barrier(jnp.sum(block_numer * factor[..., None], 2))
        return (numer / total[..., None]).reshape(-1, E).astype(jnp.bfloat16)
    context = lax.map(attend, queries.reshape(-1, FR_DEV, E)).reshape(FRAMES, E)
    biased = (frames.astype(jnp.float32) + jnp.dot(context, context_w, preferred_element_type=jnp.float32)).astype(jnp.bfloat16)
    enc_joint = jnp.dot(biased, joint_enc_w, preferred_element_type=jnp.float32).astype(jnp.bfloat16)
    step_rows = jnp.dot(pred_table[labels.reshape(-1)], pred_w, preferred_element_type=jnp.float32).astype(jnp.bfloat16).reshape(UTT, LPOS, JH)
    blank_row = jnp.dot(pred_table[0:1], pred_w, preferred_element_type=jnp.float32).astype(jnp.bfloat16)
    predictor = jnp.concatenate([jnp.broadcast_to(blank_row[None], (UTT, 1, JH)), step_rows[:, :-1]], 1)
    positions = jnp.arange(LPOS, dtype=jnp.int32)

    def joint(pair):
        enc_block, start = pair
        index = start + jnp.arange(FR_DEV, dtype=jnp.int32)
        owner = index // TLEN
        moment = index % TLEN
        joint_in = jnp.tanh(enc_block[:, None, :].astype(jnp.float32) + predictor[owner].astype(jnp.float32)).astype(jnp.bfloat16)
        logits = jnp.dot(joint_in.reshape(-1, JH), out_w, preferred_element_type=jnp.float32).reshape(FR_DEV, LPOS, V)
        peak = lax.optimization_barrier(jnp.max(logits, -1))
        norm = peak + jnp.log(lax.optimization_barrier(jnp.sum(jnp.exp(logits - peak[..., None]), -1)))
        blank = logits[..., 0] - norm
        picked = jnp.take_along_axis(logits, labels[owner][..., None], -1)[..., 0] - norm
        live = (moment < frame_lens[owner])[:, None]
        llen = label_lens[owner][:, None]
        blank = jnp.where(live & (positions[None, :] <= llen), blank, jnp.float32(0.0))
        picked = jnp.where(live & (positions[None, :] < llen), picked, jnp.float32(0.0))
        return (blank, picked)
    starts = (jnp.arange(FRAMES // FR_DEV, dtype=jnp.int32) * FR_DEV).astype(jnp.int32)
    blank, picked = lax.map(joint, (enc_joint.reshape(-1, FR_DEV, JH), starts))
    return (blank.reshape(FRAMES, LPOS), picked.reshape(FRAMES, LPOS))
```

```python
import functools
import math

import jax
import jax.numpy as jnp
from jax import lax
from jax.experimental import pallas as pl
from jax.experimental.pallas import tpu as pltpu
from jax.sharding import Mesh, PartitionSpec as P

HEADS = 4
PAD = 16
AXES = ("y", "zl", "c", "x", "zh")
PHRASE = ("y", "zl", "c")
VOCAB = ("x", "zh")
PEERS = ("y", "zl", "x", "zh")
BF = jnp.bfloat16
F32 = jnp.float32
NT = (((1,), (1,)), ((), ()))


def mm(a, b):
    return jnp.dot(a, b, preferred_element_type=F32)


def encode_local(ids, lens, phrase_table, phrase_w):
    emb = phrase_table[ids]
    mask = (jnp.arange(ids.shape[1], dtype=jnp.int32)[None, :] < lens[:, None]).astype(BF)
    summed = jnp.einsum("npe,np->ne", emb, mask, preferred_element_type=F32)
    mean = (summed / lens[:, None].astype(F32)).astype(BF)
    return jnp.tanh(mm(mean, phrase_w)).astype(BF)


def attend_kernel(used, scale, q_ref, k_ref, v_ref, o_ref):
    rows, tile = q_ref.shape[0], 256
    k, v = k_ref[...], v_ref[...]
    for start in range(0, rows, tile):
        q = q_ref[start : start + tile, :]
        scores = lax.dot_general(q, k, NT, preferred_element_type=F32) * scale
        peak = jnp.max(scores, -1, keepdims=True)
        weights = jnp.exp(scores - peak)
        total = jnp.sum(weights, -1, keepdims=True)
        part = mm(weights.astype(BF), v) / total
        rest = peak + jnp.log(total)
        groups = tile // PAD
        shape = (groups, PAD, part.shape[1])
        row = lax.broadcasted_iota(jnp.int32, shape, 1)
        lane = lax.broadcasted_iota(jnp.int32, shape, 2)
        part = part.reshape(shape)
        for piece in range(3):
            sent = rest.astype(BF).astype(F32)
            rest = rest - sent
            spread = jnp.broadcast_to(sent, (tile, shape[2])).reshape(shape)
            line = jnp.sum(jnp.where(lane == row, spread, 0.0), 1, keepdims=True)
            part = jnp.where(row == used + piece, line, part)
        o_ref[start : start + tile, :] = part.reshape(tile, shape[2]).astype(BF)


def attend(asked, keys, values, used):
    rows, width = asked.shape
    head = width // HEADS
    phrases = keys.shape[0]
    return pl.pallas_call(
        functools.partial(attend_kernel, used, 1.0 / math.sqrt(head)),
        grid=(HEADS,),
        in_specs=[
            pl.BlockSpec((rows, head), lambda h: (0, h)),
            pl.BlockSpec((phrases, head), lambda h: (0, h)),
            pl.BlockSpec((phrases, head), lambda h: (0, h)),
        ],
        out_specs=pl.BlockSpec((rows, head), lambda h: (0, h)),
        out_shape=jax.ShapeDtypeStruct((rows, width), BF),
        cost_estimate=pl.CostEstimate(
            flops=4 * rows * phrases * width,
            bytes_accessed=4 * rows * width + 4 * phrases * width,
            transcendentals=rows * phrases * HEADS,
        ),
    )(asked, keys, values)


def join_kernel(used, parts_ref, frames_ref, context_w_ref, joint_w_ref, o_ref):
    peers, pad, width = parts_ref.shape
    head = width // HEADS
    row = lax.broadcasted_iota(jnp.int32, (peers, pad, head), 1)
    lane = lax.broadcasted_iota(jnp.int32, (peers, pad, head), 2)
    columns = []
    for h in range(HEADS):
        block = parts_ref[:, :, h * head : (h + 1) * head].astype(F32)
        lse = jnp.sum(jnp.where((row >= used) & (row < used + 3), block, 0.0), 1, keepdims=True)
        factor = jnp.exp(lse - jnp.max(lse, 0, keepdims=True))
        factor = factor / jnp.sum(factor, 0, keepdims=True)
        weight = jnp.sum(jnp.where(lane == row, factor, 0.0), -1, keepdims=True)
        columns.append(jnp.sum(weight * block, 0))
    context = jnp.concatenate(columns, 1).astype(BF)
    biased = (frames_ref[...].astype(F32) + mm(context, context_w_ref[...])).astype(BF)
    o_ref[...] = mm(biased, joint_w_ref[...]).astype(BF)


def join(parts, frames, context_w, joint_w, used):
    return pl.pallas_call(
        functools.partial(join_kernel, used),
        out_shape=jax.ShapeDtypeStruct((frames.shape[0], joint_w.shape[1]), BF),
    )(parts, frames, context_w, joint_w)


def joint_kernel(used, first_ref, enc_ref, pred_ref, out_w_ref, labels_ref, o_ref, enc_s, in_s):
    groups, pad, width = enc_ref.shape
    frames = groups * used
    own = pred_ref.shape[0]
    cols = out_w_ref.shape[0]
    tile = 256

    @pl.when(pl.program_id(0) == 0)
    def _():
        for g in range(groups):
            enc_s[g * used : (g + 1) * used, :] = enc_ref[g, :used, :].astype(F32)

    for u in range(own):
        in_s[u * frames : (u + 1) * frames, :] = jnp.tanh(
            enc_s[...] + pred_ref[u : u + 1, :]
        ).astype(BF)
    column = lax.broadcasted_iota(jnp.int32, (cols, tile), 0) + first_ref[0]
    lines = tile // 128
    stat = o_ref.shape[1] // 3
    for start in range(0, own * frames, tile):
        logits = lax.dot_general(
            out_w_ref[...], in_s[start : start + tile, :], NT, preferred_element_type=F32
        )
        peak = jnp.max(logits, 0, keepdims=True)
        total = jnp.sum(jnp.exp(logits - peak), 0, keepdims=True)
        lse = peak + jnp.log(total)
        label = jnp.sum(jnp.where(column == labels_ref[0, :, start : start + tile], logits, 0.0), 0, keepdims=True)
        for i in range(lines):
            at = start // 128 + i
            piece = slice(i * 128, (i + 1) * 128)
            o_ref[0, at : at + 1, :] = lse[:, piece]
            o_ref[0, stat + at : stat + at + 1, :] = label[:, piece]
            o_ref[0, 2 * stat + at : 2 * stat + at + 1, :] = logits[0:1, piece]


def joint(enc_all, pred, out_wt, labels, first, used, n_vocab):
    groups, pad, width = enc_all.shape
    frames = groups * used
    positions = pred.shape[0]
    own = positions // n_vocab
    cols = out_wt.shape[0]
    pairs = own * frames
    stat = 8
    spread = jnp.broadcast_to(labels.reshape(n_vocab, 1, own, 1), (n_vocab, 1, own, frames))
    return pl.pallas_call(
        functools.partial(joint_kernel, used),
        grid=(n_vocab,),
        in_specs=[
            pl.BlockSpec(memory_space=pltpu.SMEM),
            pl.BlockSpec((groups, pad, width), lambda i: (0, 0, 0)),
            pl.BlockSpec((own, width), lambda i: (i, 0)),
            pl.BlockSpec((cols, width), lambda i: (0, 0)),
            pl.BlockSpec((1, 1, pairs), lambda i: (i, 0, 0)),
        ],
        out_specs=pl.BlockSpec((1, 3 * stat, 128), lambda i: (i, 0, 0)),
        out_shape=jax.ShapeDtypeStruct((n_vocab, 3 * stat, 128), F32),
        scratch_shapes=[pltpu.VMEM((frames, width), F32), pltpu.VMEM((pairs, width), BF)],
        cost_estimate=pl.CostEstimate(
            flops=2 * n_vocab * pairs * width * cols,
            bytes_accessed=2 * cols * width,
            transcendentals=n_vocab * pairs * (width + cols),
        ),
    )(first, enc_all, pred, out_wt, spread.reshape(n_vocab, 1, pairs))


def local(
    frames,
    frame_lens,
    labels,
    label_lens,
    phrase_ids,
    phrase_lens,
    phrase_table,
    phrase_w,
    key_w,
    value_w,
    query_w,
    context_w,
    joint_enc_w,
    pred_table,
    pred_w,
    out_w,
):
    n_vocab = lax.axis_size(VOCAB)
    n_phrase = lax.axis_size(PHRASE)
    n_peers = lax.axis_size(PEERS)
    used = frames.shape[0]
    frames_pad = jnp.pad(frames, ((0, PAD - used), (0, 0)))
    queries = mm(frames_pad, query_w).astype(BF)
    asked = lax.all_to_all(
        jnp.broadcast_to(queries[None], (n_peers,) + queries.shape), PEERS, 0, 0, tiled=True
    )

    phrase_vec = encode_local(phrase_ids, phrase_lens, phrase_table, phrase_w)
    other_vec = lax.ppermute(phrase_vec, "c", [(0, 1), (1, 0)])
    vecs = jnp.concatenate([phrase_vec, other_vec], 0)
    keys = mm(vecs, key_w).astype(BF)
    values = mm(vecs, value_w).astype(BF)

    utts, positions = labels.shape
    frames_dev = used * n_vocab
    tlen = frames_dev * n_phrase // utts
    start = lax.axis_index(PHRASE) * frames_dev
    utt = start // tlen
    own_labels = lax.dynamic_slice_in_dim(labels, utt, 1, 0)[0]
    picked = jnp.concatenate([jnp.zeros((1,), jnp.int32), own_labels[:-1]])
    predictor = mm(pred_table[picked], pred_w).astype(BF).astype(F32)
    out_wt = out_w.T

    parts = attend(asked.reshape(n_peers * PAD, -1), keys, values, used)
    parts = lax.all_to_all(parts.reshape(n_peers, PAD, -1), PEERS, 0, 0, tiled=True)
    enc = join(parts, frames_pad, context_w, joint_enc_w, used)
    enc_all = lax.all_to_all(
        jnp.broadcast_to(enc[None], (n_vocab,) + enc.shape), VOCAB, 0, 0, tiled=True
    )
    vocab_index = lax.axis_index(VOCAB)
    cols = out_w.shape[1]
    first = (vocab_index * cols).astype(jnp.int32).reshape(1)
    stats = joint(enc_all, predictor, out_wt, own_labels, first, used, n_vocab)
    stats = lax.all_to_all(stats, VOCAB, 0, 0, tiled=True)

    own = positions // n_vocab
    pairs = own * frames_dev
    stats = stats.reshape(n_vocab, 3, -1)[:, :, :pairs]
    lse, label, blank = stats[:, 0], stats[:, 1], stats[0, 2]
    peak = jnp.max(lse, 0)
    norm = peak + jnp.log(jnp.sum(jnp.exp(lse - peak), 0))
    label = jnp.sum(label, 0)
    moment = start % tlen + jnp.arange(frames_dev, dtype=jnp.int32)
    position = vocab_index * own + jnp.arange(own, dtype=jnp.int32)
    frame_len = lax.dynamic_slice_in_dim(frame_lens, utt, 1, 0)
    label_len = lax.dynamic_slice_in_dim(label_lens, utt, 1, 0)
    live = (moment < frame_len)[None, :]
    blank = (blank - norm).reshape(own, frames_dev)
    label = (label - norm).reshape(own, frames_dev)
    blank_out = jnp.where(live & (position <= label_len)[:, None], blank, 0.0)
    label_out = jnp.where(live & (position < label_len)[:, None], label, 0.0)
    return (blank_out.T, label_out.T)


def solution(mesh):
    n_phrase, n_vocab = mesh.devices.shape
    fine = Mesh(mesh.devices.reshape(n_phrase // 4, 2, 2, n_vocab // 2, 2), AXES)
    rows = P(AXES, None)
    in_specs = (
        rows,
        P(),
        P(),
        P(),
        rows,
        P(AXES),
        P(),
        P(),
        P(),
        P(),
        P(),
        P(),
        P(),
        P(),
        P(),
        P(None, VOCAB),
    )
    out_specs = (P(PHRASE, VOCAB), P(PHRASE, VOCAB))
    return jax.shard_map(local, mesh=fine, in_specs=in_specs, out_specs=out_specs, check_vma=False)
```

```python
import functools
import math

import jax
import jax.numpy as jnp
from jax import lax
from jax.experimental import pallas as pl
from jax.experimental.pallas import tpu as pltpu
from jax.sharding import Mesh, PartitionSpec as P

HEADS = 4
PAD = 16
AXES = ("y", "zl", "c", "x", "zh")
PHRASE = ("y", "zl", "c")
VOCAB = ("x", "zh")
PEERS = ("y", "zl", "x", "zh")
BF = jnp.bfloat16
F32 = jnp.float32
LOG2E = 1.0 / math.log(2.0)
NT = (((1,), (1,)), ((), ()))


def mm(a, b):
    return jnp.dot(a, b, preferred_element_type=F32)


def encode_kernel(ids_ref, lens_ref, table_ref, phrase_w_ref, key_w_ref, value_w_ref, k_ref, v_ref):
    rows, tokens = ids_ref.shape
    vocab = table_ref.shape[0]
    lens = lens_ref[...]
    slot = lax.broadcasted_iota(jnp.int32, (rows, tokens), 1)
    ids = jnp.where(slot < lens, ids_ref[...], -1)
    lane = lax.broadcasted_iota(jnp.int32, (rows, 128), 1)
    blocks, units = [], []
    for t in range(tokens):
        token = jnp.broadcast_to(ids[:, t : t + 1], (rows, 128))
        blocks.append(lax.shift_right_arithmetic(token, 7).astype(F32).astype(BF))
        units.append(jnp.where((token & 127) == lane, 1.0, 0.0).astype(BF))
    zero = jnp.zeros((rows, 128), BF)
    summed = jnp.zeros((rows, table_ref.shape[1]), F32)
    for pair in range(vocab // 256):
        counts = []
        for block in (2 * pair, 2 * pair + 1):
            count = zero
            for t in range(tokens):
                count += jnp.where(blocks[t] == BF(block), units[t], zero)
            counts.append(count)
        summed += mm(jnp.concatenate(counts, 1), table_ref[pair * 256 : (pair + 1) * 256, :])
    mean = (summed / lens.astype(F32)).astype(BF)
    vec = jnp.tanh(mm(mean, phrase_w_ref[...])).astype(BF)
    k_ref[...] = mm(vec, key_w_ref[...]).astype(BF)
    v_ref[...] = mm(vec, value_w_ref[...]).astype(BF)


def encode(ids, lens, table, phrase_w, key_w, value_w):
    phrases, tokens = ids.shape
    vocab, width = table.shape
    tile = 256
    whole = lambda a: pl.BlockSpec(a.shape, lambda i: (0, 0))
    return pl.pallas_call(
        encode_kernel,
        grid=(phrases // tile,),
        in_specs=[
            pl.BlockSpec((tile, tokens), lambda i: (i, 0)),
            pl.BlockSpec((tile, 1), lambda i: (i, 0)),
            whole(table),
            whole(phrase_w),
            whole(key_w),
            whole(value_w),
        ],
        out_specs=[pl.BlockSpec((tile, width), lambda i: (i, 0))] * 2,
        out_shape=[jax.ShapeDtypeStruct((phrases, width), BF)] * 2,
        cost_estimate=pl.CostEstimate(
            flops=40 * phrases * vocab * width,
            bytes_accessed=2 * vocab * width,
            transcendentals=phrases * width,
        ),
    )(ids, lens.reshape(-1, 1), table, phrase_w, key_w, value_w)


def attend_kernel(used, scale, q_ref, k_ref, v_ref, o_ref):
    rows, tile = q_ref.shape[0], 256
    k, v = k_ref[...], v_ref[...]
    head = v.shape[1]
    v_ones = jnp.concatenate([v, jnp.ones_like(v)], 1)
    for start in range(0, rows, tile):
        q = q_ref[start : start + tile, :]
        scores = lax.dot_general(q, k, NT, preferred_element_type=F32)
        peak = jnp.max(scores, -1, keepdims=True)
        weights = jnp.exp2((scores - peak) * (scale * LOG2E)).astype(BF)
        sums = mm(weights, v_ones)
        total = sums[:, head:]
        part = sums[:, :head] / total
        rest = peak * scale + jnp.log(total)
        groups = tile // PAD
        shape = (groups, PAD, part.shape[1])
        row = lax.broadcasted_iota(jnp.int32, shape, 1)
        lane = lax.broadcasted_iota(jnp.int32, shape, 2)
        part = part.reshape(shape)
        for piece in range(3):
            sent = rest.astype(BF).astype(F32)
            rest = rest - sent
            line = jnp.sum(jnp.where(lane == row, sent.reshape(shape), 0.0), 1, keepdims=True)
            part = jnp.where(row == used + piece, line, part)
        o_ref[start : start + tile, :] = part.reshape(tile, shape[2]).astype(BF)


def attend(asked, keys, values, used):
    rows, width = asked.shape
    head = width // HEADS
    phrases = keys.shape[0]
    return pl.pallas_call(
        functools.partial(attend_kernel, used, 1.0 / math.sqrt(head)),
        grid=(HEADS,),
        in_specs=[
            pl.BlockSpec((rows, head), lambda h: (0, h)),
            pl.BlockSpec((phrases, head), lambda h: (0, h)),
            pl.BlockSpec((phrases, head), lambda h: (0, h)),
        ],
        out_specs=pl.BlockSpec((rows, head), lambda h: (0, h)),
        out_shape=jax.ShapeDtypeStruct((rows, width), BF),
        cost_estimate=pl.CostEstimate(
            flops=4 * rows * phrases * width,
            bytes_accessed=4 * rows * width + 4 * phrases * width,
            transcendentals=rows * phrases * HEADS,
        ),
    )(asked, keys, values)


def join_kernel(used, parts_ref, frames_ref, context_w_ref, joint_w_ref, o_ref):
    peers, pad, width = parts_ref.shape
    head = width // HEADS
    row = lax.broadcasted_iota(jnp.int32, (peers, pad, head), 1)
    lane = lax.broadcasted_iota(jnp.int32, (peers, pad, head), 2)
    columns = []
    for h in range(HEADS):
        block = parts_ref[:, :, h * head : (h + 1) * head].astype(F32)
        lse = jnp.sum(jnp.where((row >= used) & (row < used + 3), block, 0.0), 1, keepdims=True)
        factor = jnp.exp(lse - jnp.max(lse, 0, keepdims=True))
        factor = factor / jnp.sum(factor, 0, keepdims=True)
        weight = jnp.sum(jnp.where(lane == row, factor, 0.0), -1, keepdims=True)
        columns.append(jnp.sum(weight * block, 0))
    context = jnp.concatenate(columns, 1).astype(BF)
    biased = (frames_ref[...].astype(F32) + mm(context, context_w_ref[...])).astype(BF)
    joint_rows = mm(biased, joint_w_ref[...]).astype(BF)
    for i in range(o_ref.shape[0]):
        o_ref[i] = joint_rows


def join(parts, frames, context_w, joint_w, used, copies):
    return pl.pallas_call(
        functools.partial(join_kernel, used),
        out_shape=jax.ShapeDtypeStruct((copies, frames.shape[0], joint_w.shape[1]), BF),
    )(parts, frames, context_w, joint_w)


def joint_kernel(used, enc_ref, pred_ref, out_w_ref, label_w_ref, o_ref, enc_s, w_s):
    groups, pad, width = enc_ref.shape
    frames = groups * used
    own = pred_ref.shape[0]
    cols = out_w_ref.shape[0]
    tile = 256

    @pl.when(pl.program_id(0) == 0)
    def _():
        for g in range(groups):
            enc_s[g * used : (g + 1) * used, :] = enc_ref[g, :used, :].astype(F32)
        w_s[:cols, :] = out_w_ref[...]

    w_s[cols:, :] = label_w_ref[0]
    pred = pred_ref[...]
    stat = o_ref.shape[1] // 3
    for start in range(0, own * frames, tile):
        pieces, at = [], start
        while at < start + tile:
            u, f = at // frames, at % frames
            size = min(frames - f, start + tile - at)
            pieces.append(jnp.tanh(enc_s[f : f + size, :] + pred[u : u + 1, :]).astype(BF))
            at += size
        rows = jnp.concatenate(pieces, 0)
        found = lax.dot_general(w_s[...], rows, NT, preferred_element_type=F32)
        logits = found[:cols]
        peak = jnp.max(logits, 0, keepdims=True)
        total = jnp.sum(jnp.exp2((logits - peak) * LOG2E), 0, keepdims=True)
        lse = peak + jnp.log(total)
        pair = lax.broadcasted_iota(jnp.int32, (own, tile), 1) + start
        low = lax.broadcasted_iota(jnp.int32, (own, tile), 0) * frames
        mine = (pair >= low) & (pair < low + frames)
        label = jnp.sum(jnp.where(mine, found[cols : cols + own], 0.0), 0, keepdims=True)
        for i in range(tile // 128):
            at = start // 128 + i
            piece = slice(i * 128, (i + 1) * 128)
            o_ref[0, at : at + 1, :] = lse[:, piece]
            o_ref[0, stat + at : stat + at + 1, :] = label[:, piece]
            o_ref[0, 2 * stat + at : 2 * stat + at + 1, :] = logits[0:1, piece]


def joint(enc_all, pred, out_wt, label_w, used, n_vocab):
    groups, pad, width = enc_all.shape
    frames = groups * used
    own = pred.shape[0] // n_vocab
    cols = out_wt.shape[0]
    pairs = own * frames
    stat = 8
    label_w = jnp.pad(label_w.reshape(n_vocab, own, width), ((0, 0), (0, 16 - own), (0, 0)))
    return pl.pallas_call(
        functools.partial(joint_kernel, used),
        grid=(n_vocab,),
        in_specs=[
            pl.BlockSpec((groups, pad, width), lambda i: (0, 0, 0)),
            pl.BlockSpec((own, width), lambda i: (i, 0)),
            pl.BlockSpec((cols, width), lambda i: (0, 0)),
            pl.BlockSpec((1, 16, width), lambda i: (i, 0, 0)),
        ],
        out_specs=pl.BlockSpec((1, 3 * stat, 128), lambda i: (i, 0, 0)),
        out_shape=jax.ShapeDtypeStruct((n_vocab, 3 * stat, 128), F32),
        scratch_shapes=[pltpu.VMEM((frames, width), F32), pltpu.VMEM((cols + 16, width), BF)],
        cost_estimate=pl.CostEstimate(
            flops=2 * n_vocab * pairs * width * cols,
            bytes_accessed=2 * cols * width,
            transcendentals=n_vocab * pairs * (width + cols),
        ),
    )(enc_all, pred, out_wt, label_w)


def local(
    frames,
    frame_lens,
    labels,
    label_lens,
    phrase_ids,
    phrase_lens,
    phrase_table,
    phrase_w,
    key_w,
    value_w,
    query_w,
    context_w,
    joint_enc_w,
    pred_table,
    pred_w,
    out_w,
):
    n_vocab = lax.axis_size(VOCAB)
    n_phrase = lax.axis_size(PHRASE)
    n_peers = lax.axis_size(PEERS)
    used = frames.shape[0]
    frames_pad = jnp.pad(frames, ((0, PAD - used), (0, 0)))
    queries = mm(frames_pad, query_w).astype(BF)
    asked = lax.all_to_all(
        jnp.broadcast_to(queries[None], (n_peers,) + queries.shape), PEERS, 0, 0, tiled=True
    )

    swap = [(0, 1), (1, 0)]
    ids = jnp.concatenate([phrase_ids, lax.ppermute(phrase_ids, "c", swap)], 0)
    lens = jnp.concatenate([phrase_lens, lax.ppermute(phrase_lens, "c", swap)], 0)
    keys, values = encode(ids, lens, phrase_table, phrase_w, key_w, value_w)

    utts, positions = labels.shape
    frames_dev = used * n_vocab
    tlen = frames_dev * n_phrase // utts
    start = lax.axis_index(PHRASE) * frames_dev
    utt = start // tlen
    own_labels = lax.dynamic_slice_in_dim(labels, utt, 1, 0)[0]
    picked = jnp.concatenate([jnp.zeros((1,), jnp.int32), own_labels[:-1]])
    predictor = mm(pred_table[picked], pred_w).astype(BF).astype(F32)
    vocab_index = lax.axis_index(VOCAB)
    cols = out_w.shape[1]
    out_wt = out_w.T
    column = vocab_index * cols + jnp.arange(cols, dtype=jnp.int32)
    label_w = mm((own_labels[:, None] == column[None, :]).astype(BF), out_wt).astype(BF)

    parts = attend(asked.reshape(n_peers * PAD, -1), keys, values, used)
    parts = lax.all_to_all(parts.reshape(n_peers, PAD, -1), PEERS, 0, 0, tiled=True)
    enc = join(parts, frames_pad, context_w, joint_enc_w, used, n_vocab)
    enc_all = lax.all_to_all(enc, VOCAB, 0, 0, tiled=True)
    stats = joint(enc_all, predictor, out_wt, label_w, used, n_vocab)
    stats = lax.all_to_all(stats, VOCAB, 0, 0, tiled=True)

    own = positions // n_vocab
    pairs = own * frames_dev
    stats = stats.reshape(n_vocab, 3, -1)[:, :, :pairs]
    lse, label, blank = stats[:, 0], stats[:, 1], stats[0, 2]
    peak = jnp.max(lse, 0)
    norm = peak + jnp.log(jnp.sum(jnp.exp(lse - peak), 0))
    label = jnp.sum(label, 0)
    moment = start % tlen + jnp.arange(frames_dev, dtype=jnp.int32)
    position = vocab_index * own + jnp.arange(own, dtype=jnp.int32)
    frame_len = lax.dynamic_slice_in_dim(frame_lens, utt, 1, 0)
    label_len = lax.dynamic_slice_in_dim(label_lens, utt, 1, 0)
    live = (moment < frame_len)[None, :]
    blank = (blank - norm).reshape(own, frames_dev)
    label = (label - norm).reshape(own, frames_dev)
    blank_out = jnp.where(live & (position <= label_len)[:, None], blank, 0.0)
    label_out = jnp.where(live & (position < label_len)[:, None], label, 0.0)
    return (blank_out.T, label_out.T)


def solution(mesh):
    n_phrase, n_vocab = mesh.devices.shape
    fine = Mesh(mesh.devices.reshape(n_phrase // 4, 2, 2, n_vocab // 2, 2), AXES)
    rows = P(AXES, None)
    in_specs = (
        rows,
        P(),
        P(),
        P(),
        rows,
        P(AXES),
        P(),
        P(),
        P(),
        P(),
        P(),
        P(),
        P(),
        P(),
        P(),
        P(None, VOCAB),
    )
    out_specs = (P(PHRASE, VOCAB), P(PHRASE, VOCAB))
    return jax.shard_map(local, mesh=fine, in_specs=in_specs, out_specs=out_specs, check_vma=False)
```

```python
import functools
import math

import jax
import jax.numpy as jnp
from jax import lax
from jax.experimental import pallas as pl
from jax.experimental.pallas import tpu as pltpu
from jax.sharding import Mesh, PartitionSpec as P

HEADS = 4
PAD = 16
AXES = ("y", "zl", "c", "x", "zh")
PHRASE = ("y", "zl", "c")
VOCAB = ("x", "zh")
PEERS = ("y", "zl", "x", "zh")
BF = jnp.bfloat16
F32 = jnp.float32
LOG2E = 1.0 / math.log(2.0)
NT = (((1,), (1,)), ((), ()))


def mm(a, b):
    return jnp.dot(a, b, preferred_element_type=F32)


def encode_kernel(ids_ref, table_ref, phrase_w_ref, key_w_ref, value_w_ref, o_ref):
    rows, tokens = ids_ref.shape
    vocab = table_ref.shape[0]
    ids = ids_ref[...]
    lens = jnp.sum(jnp.where(ids >= 0, 1.0, 0.0), 1, keepdims=True)
    lane = lax.broadcasted_iota(jnp.int32, (rows, 128), 1)
    blocks, units = [], []
    for t in range(tokens):
        token = jnp.broadcast_to(ids[:, t : t + 1], (rows, 128))
        blocks.append(lax.shift_right_arithmetic(token, 7).astype(F32).astype(BF))
        units.append(jnp.where((token & 127) == lane, 1.0, 0.0).astype(BF))
    zero = jnp.zeros((rows, 128), BF)
    summed = jnp.zeros((rows, table_ref.shape[1]), F32)
    for pair in range(vocab // 256):
        counts = []
        for block in (2 * pair, 2 * pair + 1):
            count = zero
            for t in range(tokens):
                count += jnp.where(blocks[t] == BF(block), units[t], zero)
            counts.append(count)
        summed += mm(jnp.concatenate(counts, 1), table_ref[pair * 256 : (pair + 1) * 256, :])
    mean = (summed / lens).astype(BF)
    vec = jnp.tanh(mm(mean, phrase_w_ref[...])).astype(BF)
    width = key_w_ref.shape[1]
    o_ref[:, :width] = mm(vec, key_w_ref[...]).astype(BF)
    o_ref[:, width:] = mm(vec, value_w_ref[...]).astype(BF)


def encode(ids, table, phrase_w, key_w, value_w):
    phrases, tokens = ids.shape
    vocab, width = table.shape
    tile = 256
    whole = lambda a: pl.BlockSpec(a.shape, lambda i: (0, 0))
    return pl.pallas_call(
        encode_kernel,
        grid=(phrases // tile,),
        in_specs=[
            pl.BlockSpec((tile, tokens), lambda i: (i, 0)),
            whole(table),
            whole(phrase_w),
            whole(key_w),
            whole(value_w),
        ],
        out_specs=pl.BlockSpec((tile, 2 * width), lambda i: (i, 0)),
        out_shape=jax.ShapeDtypeStruct((phrases, 2 * width), BF),
        cost_estimate=pl.CostEstimate(
            flops=40 * phrases * vocab * width,
            bytes_accessed=2 * vocab * width,
            transcendentals=phrases * width,
        ),
    )(ids, table, phrase_w, key_w, value_w)


def attend_kernel(used, scale, q_ref, k0_ref, v0_ref, k1_ref, v1_ref, o_ref):
    rows, tile = q_ref.shape[0], 256
    k = jnp.concatenate([k0_ref[...], k1_ref[...]], 0)
    v = jnp.concatenate([v0_ref[...], v1_ref[...]], 0)
    head = v.shape[1]
    v_ones = jnp.concatenate([v, jnp.ones_like(v)], 1)
    for start in range(0, rows, tile):
        q = q_ref[start : start + tile, :]
        scores = lax.dot_general(q, k, NT, preferred_element_type=F32)
        peak = jnp.max(scores, -1, keepdims=True)
        weights = jnp.exp2((scores - peak) * (scale * LOG2E)).astype(BF)
        sums = mm(weights, v_ones)
        total = sums[:, head:]
        part = sums[:, :head] / total
        rest = peak * scale + jnp.log(total)
        groups = tile // PAD
        shape = (groups, PAD, part.shape[1])
        row = lax.broadcasted_iota(jnp.int32, shape, 1)
        lane = lax.broadcasted_iota(jnp.int32, shape, 2)
        part = part.reshape(shape)
        for piece in range(3):
            sent = rest.astype(BF).astype(F32)
            rest = rest - sent
            line = jnp.sum(jnp.where(lane == row, sent.reshape(shape), 0.0), 1, keepdims=True)
            part = jnp.where(row == used + piece, line, part)
        o_ref[start : start + tile, :] = part.reshape(tile, shape[2]).astype(BF)


def attend(asked, both, other, used):
    rows, width = asked.shape
    head = width // HEADS
    phrases = both.shape[0]
    keys = pl.BlockSpec((phrases, head), lambda h: (0, h))
    values = pl.BlockSpec((phrases, head), lambda h: (0, HEADS + h))
    return pl.pallas_call(
        functools.partial(attend_kernel, used, 1.0 / math.sqrt(head)),
        grid=(HEADS,),
        in_specs=[
            pl.BlockSpec((rows, head), lambda h: (0, h)),
            keys,
            values,
            keys,
            values,
        ],
        out_specs=pl.BlockSpec((rows, head), lambda h: (0, h)),
        out_shape=jax.ShapeDtypeStruct((rows, width), BF),
        cost_estimate=pl.CostEstimate(
            flops=8 * rows * phrases * width,
            bytes_accessed=4 * rows * width + 8 * phrases * width,
            transcendentals=2 * rows * phrases * HEADS,
        ),
    )(asked, both, both, other, other)


def joint_kernel(
    used, parts_ref, frames_ref, context_w_ref, joint_w_ref, pred_ref, label_w_ref, w_ref, o_ref,
    rows_s, lse_s, found_s,
):
    step = pl.program_id(0)
    count = rows_s.shape[0]
    positions = pred_ref.shape[0]
    groups = o_ref.shape[0]
    own = positions // groups
    pairs = own * used

    @pl.when(step == 0)
    def _():
        peers, pad, width = parts_ref.shape
        head = width // HEADS
        row = lax.broadcasted_iota(jnp.int32, (peers, pad, head), 1)
        lane = lax.broadcasted_iota(jnp.int32, (peers, pad, head), 2)
        columns = []
        for h in range(HEADS):
            block = parts_ref[:, :, h * head : (h + 1) * head].astype(F32)
            lse = jnp.sum(jnp.where((row >= used) & (row < used + 3), block, 0.0), 1, keepdims=True)
            factor = jnp.exp(lse - jnp.max(lse, 0, keepdims=True))
            factor = factor / jnp.sum(factor, 0, keepdims=True)
            weight = jnp.sum(jnp.where(lane == row, factor, 0.0), -1, keepdims=True)
            columns.append(jnp.sum(weight * block, 0))
        context = jnp.concatenate(columns, 1).astype(BF)
        biased = (frames_ref[...].astype(F32) + mm(context, context_w_ref[...])).astype(BF)
        enc = mm(biased, joint_w_ref[...]).astype(BF).astype(F32)
        for g in range(groups):
            pred = pred_ref[g * own : (g + 1) * own, :]
            for f in range(0, used, 2):
                pair = jnp.concatenate([pred + enc[f : f + 1, :], pred + enc[f + 1 : f + 2, :]], 0)
                at = g * pairs + f * own
                rows_s[at : at + 2 * own, :] = jnp.tanh(pair).astype(BF)
        found = lax.dot_general(label_w_ref[...], rows_s[...], NT, preferred_element_type=F32)
        at = lax.broadcasted_iota(jnp.int32, found.shape, 1)
        position = (at // pairs) * own + at % own
        mine = position == lax.broadcasted_iota(jnp.int32, found.shape, 0)
        found_s[0:1, :] = jnp.sum(jnp.where(mine, found, 0.0), 0, keepdims=True)

    tile = 256
    for start in range(0, count, tile):
        rows = rows_s[start : start + tile, :]
        logits = lax.dot_general(w_ref[...], rows, NT, preferred_element_type=F32)
        peak = jnp.max(logits, 0, keepdims=True)
        total = jnp.sum(jnp.exp2((logits - peak) * LOG2E), 0, keepdims=True)
        lse_s[pl.ds(step, 1), start : start + tile] = peak + jnp.log(total)

        @pl.when(step == 0)
        def _():
            found_s[1:2, start : start + tile] = logits[0:1]

    @pl.when(step == pl.num_programs(0) - 1)
    def _():
        lse = lse_s[...]
        peak = jnp.max(lse, 0, keepdims=True)
        norm = peak + jnp.log(jnp.sum(jnp.exp(lse - peak), 0, keepdims=True))
        label = found_s[0:1, :] - norm
        blank = found_s[1:2, :] - norm
        for g in range(groups):
            piece = slice(g * pairs, (g + 1) * pairs)
            o_ref[g, 0:1, :pairs] = blank[:, piece]
            o_ref[g, 1:2, :pairs] = label[:, piece]


def joint(parts, frames, context_w, joint_w, pred, label_w, out_wt, used, groups):
    vocab, width = out_wt.shape
    positions = pred.shape[0]
    count = positions * used
    block = 512
    whole = lambda a: pl.BlockSpec(a.shape, lambda i: (0,) * a.ndim)
    return pl.pallas_call(
        functools.partial(joint_kernel, used),
        grid=(vocab // block,),
        in_specs=[whole(a) for a in (parts, frames, context_w, joint_w, pred, label_w)]
        + [pl.BlockSpec((block, width), lambda i: (i, 0))],
        out_specs=pl.BlockSpec((groups, 2, 128), lambda i: (0, 0, 0)),
        out_shape=jax.ShapeDtypeStruct((groups, 2, 128), F32),
        scratch_shapes=[
            pltpu.VMEM((count, width), BF),
            pltpu.VMEM((vocab // block, count), F32),
            pltpu.VMEM((8, count), F32),
        ],
        cost_estimate=pl.CostEstimate(
            flops=2 * count * width * vocab,
            bytes_accessed=2 * vocab * width,
            transcendentals=count * vocab,
        ),
    )(parts, frames, context_w, joint_w, pred, label_w, out_wt)


def local(
    frames,
    frame_lens,
    labels,
    label_lens,
    phrase_ids,
    phrase_lens,
    phrase_table,
    phrase_w,
    key_w,
    value_w,
    query_w,
    context_w,
    joint_enc_w,
    pred_table,
    pred_w,
    out_w,
):
    n_vocab = lax.axis_size(VOCAB)
    n_phrase = lax.axis_size(PHRASE)
    n_peers = lax.axis_size(PEERS)
    used = frames.shape[0]
    out_wt = lax.all_gather(out_w.T, VOCAB, axis=0, tiled=True)
    frames_pad = jnp.pad(frames, ((0, PAD - used), (0, 0)))
    queries = mm(frames_pad, query_w).astype(BF)
    asked = lax.all_to_all(
        jnp.broadcast_to(queries[None], (n_peers,) + queries.shape), PEERS, 0, 0, tiled=True
    )

    swap = [(0, 1), (1, 0)]
    slot = jnp.arange(phrase_ids.shape[1], dtype=jnp.int32)
    ids = jnp.where(slot[None, :] < phrase_lens[:, None], phrase_ids, -1)
    both = encode(ids, phrase_table, phrase_w, key_w, value_w)
    other = lax.ppermute(both, "c", swap)

    utts, positions = labels.shape
    frames_dev = used * n_vocab
    tlen = frames_dev * n_phrase // utts
    start = lax.axis_index(PHRASE) * frames_dev
    utt = start // tlen
    own_labels = lax.dynamic_slice_in_dim(labels, utt, 1, 0)[0]
    picked = jnp.concatenate([jnp.zeros((1,), jnp.int32), own_labels[:-1]])
    predictor = mm(pred_table[picked], pred_w).astype(BF).astype(F32)
    label_w = out_wt[own_labels]

    parts = attend(asked.reshape(n_peers * PAD, -1), both, other, used)
    parts = lax.all_to_all(parts.reshape(n_peers, PAD, -1), PEERS, 0, 0, tiled=True)
    logp = joint(
        parts, frames_pad, context_w, joint_enc_w, predictor, label_w, out_wt, used, n_vocab
    )
    logp = lax.all_to_all(logp, VOCAB, 0, 0, tiled=True)

    own = positions // n_vocab
    logp = logp[:, :, : own * used].reshape(n_vocab, 2, used, own)
    blank = logp[:, 0].reshape(frames_dev, own)
    label = logp[:, 1].reshape(frames_dev, own)
    moment = start % tlen + jnp.arange(frames_dev, dtype=jnp.int32)
    position = lax.axis_index(VOCAB) * own + jnp.arange(own, dtype=jnp.int32)
    frame_len = lax.dynamic_slice_in_dim(frame_lens, utt, 1, 0)
    label_len = lax.dynamic_slice_in_dim(label_lens, utt, 1, 0)
    live = (moment < frame_len)[:, None]
    blank_out = jnp.where(live & (position <= label_len)[None, :], blank, 0.0)
    label_out = jnp.where(live & (position < label_len)[None, :], label, 0.0)
    return (blank_out, label_out)


def solution(mesh):
    n_phrase, n_vocab = mesh.devices.shape
    fine = Mesh(mesh.devices.reshape(n_phrase // 4, 2, 2, n_vocab // 2, 2), AXES)
    rows = P(AXES, None)
    in_specs = (
        rows,
        P(),
        P(),
        P(),
        rows,
        P(AXES),
        P(),
        P(),
        P(),
        P(),
        P(),
        P(),
        P(),
        P(),
        P(),
        P(None, VOCAB),
    )
    out_specs = (P(PHRASE, VOCAB), P(PHRASE, VOCAB))
    return jax.shard_map(local, mesh=fine, in_specs=in_specs, out_specs=out_specs, check_vma=False)
```

```python
import functools
import math

import jax
import jax.numpy as jnp
from jax import lax
from jax.experimental import pallas as pl
from jax.experimental.pallas import tpu as pltpu
from jax.sharding import Mesh, PartitionSpec as P

HEADS = 4
PAD = 16
AXES = ("y", "zl", "c", "x", "zh")
PHRASE = ("y", "zl", "c")
VOCAB = ("x", "zh")
PEERS = ("y", "zl", "x", "zh")
BF = jnp.bfloat16
F32 = jnp.float32
LOG2E = 1.0 / math.log(2.0)
NT = (((1,), (1,)), ((), ()))


def mm(a, b):
    return jnp.dot(a, b, preferred_element_type=F32)


def encode_kernel(ids_ref, table_ref, phrase_w_ref, key_w_ref, value_w_ref, k_ref, v_ref):
    rows, tokens = ids_ref.shape
    vocab = table_ref.shape[0]
    ids = ids_ref[...]
    lens = jnp.sum(jnp.where(ids >= 0, 1.0, 0.0), 1, keepdims=True)
    lane = lax.broadcasted_iota(jnp.int32, (rows, 128), 1)
    blocks, units = [], []
    for t in range(tokens):
        token = jnp.broadcast_to(ids[:, t : t + 1], (rows, 128))
        blocks.append(lax.shift_right_arithmetic(token, 7).astype(F32).astype(BF))
        units.append(jnp.where((token & 127) == lane, 1.0, 0.0).astype(BF))
    zero = jnp.zeros((rows, 128), BF)
    summed = jnp.zeros((rows, table_ref.shape[1]), F32)
    for pair in range(vocab // 256):
        counts = []
        for block in (2 * pair, 2 * pair + 1):
            count = zero
            for t in range(tokens):
                count += jnp.where(blocks[t] == BF(block), units[t], zero)
            counts.append(count)
        summed += mm(jnp.concatenate(counts, 1), table_ref[pair * 256 : (pair + 1) * 256, :])
    mean = (summed / lens).astype(BF)
    vec = jnp.tanh(mm(mean, phrase_w_ref[...])).astype(BF)
    k_ref[...] = mm(vec, key_w_ref[...]).astype(BF)
    v_ref[...] = mm(vec, value_w_ref[...]).astype(BF)


def encode(ids, table, phrase_w, key_w, value_w):
    phrases, tokens = ids.shape
    vocab, width = table.shape
    tile = 256
    whole = lambda a: pl.BlockSpec(a.shape, lambda i: (0, 0))
    return pl.pallas_call(
        encode_kernel,
        grid=(phrases // tile,),
        in_specs=[
            pl.BlockSpec((tile, tokens), lambda i: (i, 0)),
            whole(table),
            whole(phrase_w),
            whole(key_w),
            whole(value_w),
        ],
        out_specs=[pl.BlockSpec((tile, width), lambda i: (i, 0))] * 2,
        out_shape=[jax.ShapeDtypeStruct((phrases, width), BF)] * 2,
        cost_estimate=pl.CostEstimate(
            flops=40 * phrases * vocab * width,
            bytes_accessed=2 * vocab * width,
            transcendentals=phrases * width,
        ),
    )(ids, table, phrase_w, key_w, value_w)


def attend_kernel(used, scale, q_ref, k0_ref, v0_ref, k1_ref, v1_ref, o_ref):
    rows, tile = q_ref.shape[0], 256
    k = jnp.concatenate([k0_ref[...], k1_ref[...]], 0)
    v = jnp.concatenate([v0_ref[...], v1_ref[...]], 0)
    head = v.shape[1]
    v_ones = jnp.concatenate([v, jnp.ones_like(v)], 1)
    for start in range(0, rows, tile):
        q = q_ref[start : start + tile, :]
        scores = lax.dot_general(q, k, NT, preferred_element_type=F32)
        peak = jnp.max(scores, -1, keepdims=True)
        weights = jnp.exp2((scores - peak) * (scale * LOG2E)).astype(BF)
        sums = mm(weights, v_ones)
        total = sums[:, head:]
        part = sums[:, :head] / total
        rest = peak * scale + jnp.log(total)
        groups = tile // PAD
        shape = (groups, PAD, part.shape[1])
        row = lax.broadcasted_iota(jnp.int32, shape, 1)
        lane = lax.broadcasted_iota(jnp.int32, shape, 2)
        part = part.reshape(shape)
        for piece in range(3):
            sent = rest.astype(BF).astype(F32)
            rest = rest - sent
            line = jnp.sum(jnp.where(lane == row, sent.reshape(shape), 0.0), 1, keepdims=True)
            part = jnp.where(row == used + piece, line, part)
        o_ref[start : start + tile, :] = part.reshape(tile, shape[2]).astype(BF)


def attend(asked, keys, values, other_keys, other_values, used):
    rows, width = asked.shape
    head = width // HEADS
    phrases = keys.shape[0]
    part = pl.BlockSpec((phrases, head), lambda h: (0, h))
    return pl.pallas_call(
        functools.partial(attend_kernel, used, 1.0 / math.sqrt(head)),
        grid=(HEADS,),
        in_specs=[
            pl.BlockSpec((rows, head), lambda h: (0, h)),
            part,
            part,
            part,
            part,
        ],
        out_specs=pl.BlockSpec((rows, head), lambda h: (0, h)),
        out_shape=jax.ShapeDtypeStruct((rows, width), BF),
        cost_estimate=pl.CostEstimate(
            flops=8 * rows * phrases * width,
            bytes_accessed=4 * rows * width + 8 * phrases * width,
            transcendentals=2 * rows * phrases * HEADS,
        ),
    )(asked, keys, values, other_keys, other_values)


def join_kernel(used, parts_ref, frames_ref, context_w_ref, joint_w_ref, o_ref):
    peers, pad, width = parts_ref.shape
    head = width // HEADS
    row = lax.broadcasted_iota(jnp.int32, (peers, pad, head), 1)
    lane = lax.broadcasted_iota(jnp.int32, (peers, pad, head), 2)
    columns = []
    for h in range(HEADS):
        block = parts_ref[:, :, h * head : (h + 1) * head].astype(F32)
        lse = jnp.sum(jnp.where((row >= used) & (row < used + 3), block, 0.0), 1, keepdims=True)
        factor = jnp.exp(lse - jnp.max(lse, 0, keepdims=True))
        factor = factor / jnp.sum(factor, 0, keepdims=True)
        weight = jnp.sum(jnp.where(lane == row, factor, 0.0), -1, keepdims=True)
        columns.append(jnp.sum(weight * block, 0))
    context = jnp.concatenate(columns, 1).astype(BF)
    biased = (frames_ref[...].astype(F32) + mm(context, context_w_ref[...])).astype(BF)
    joint_rows = mm(biased, joint_w_ref[...]).astype(BF)
    for i in range(o_ref.shape[0]):
        o_ref[i] = joint_rows


def join(parts, frames, context_w, joint_w, used, copies):
    return pl.pallas_call(
        functools.partial(join_kernel, used),
        out_shape=jax.ShapeDtypeStruct((copies, frames.shape[0], joint_w.shape[1]), BF),
    )(parts, frames, context_w, joint_w)


def joint_kernel(used, enc_ref, pred_ref, out_w_ref, label_w_ref, o_ref, enc_s, w_s):
    groups, pad, width = enc_ref.shape
    frames = groups * used
    own = pred_ref.shape[0]
    cols = out_w_ref.shape[0]
    tile = 256

    @pl.when(pl.program_id(0) == 0)
    def _():
        for g in range(groups):
            enc_s[g * used : (g + 1) * used, :] = enc_ref[g, :used, :].astype(F32)
        w_s[:cols, :] = out_w_ref[...]

    w_s[cols:, :] = label_w_ref[0]
    pred = pred_ref[...]
    stat = o_ref.shape[1] // 3
    for start in range(0, own * frames, tile):
        pieces, at = [], start
        while at < start + tile:
            u, f = at // frames, at % frames
            size = min(frames - f, start + tile - at)
            pieces.append(jnp.tanh(enc_s[f : f + size, :] + pred[u : u + 1, :]).astype(BF))
            at += size
        rows = jnp.concatenate(pieces, 0)
        found = lax.dot_general(w_s[...], rows, NT, preferred_element_type=F32)
        logits = found[:cols]
        peak = jnp.max(logits, 0, keepdims=True)
        total = jnp.sum(jnp.exp2((logits - peak) * LOG2E), 0, keepdims=True)
        lse = peak + jnp.log(total)
        pair = lax.broadcasted_iota(jnp.int32, (own, tile), 1) + start
        low = lax.broadcasted_iota(jnp.int32, (own, tile), 0) * frames
        mine = (pair >= low) & (pair < low + frames)
        label = jnp.sum(jnp.where(mine, found[cols : cols + own], 0.0), 0, keepdims=True)
        for i in range(tile // 128):
            at = start // 128 + i
            piece = slice(i * 128, (i + 1) * 128)
            o_ref[0, at : at + 1, :] = lse[:, piece]
            o_ref[0, stat + at : stat + at + 1, :] = label[:, piece]
            o_ref[0, 2 * stat + at : 2 * stat + at + 1, :] = logits[0:1, piece]


def joint(enc_all, pred, out_wt, label_w, used, n_vocab):
    groups, pad, width = enc_all.shape
    frames = groups * used
    own = pred.shape[0] // n_vocab
    cols = out_wt.shape[0]
    pairs = own * frames
    stat = 8
    label_w = jnp.pad(label_w.reshape(n_vocab, own, width), ((0, 0), (0, 16 - own), (0, 0)))
    return pl.pallas_call(
        functools.partial(joint_kernel, used),
        grid=(n_vocab,),
        in_specs=[
            pl.BlockSpec((groups, pad, width), lambda i: (0, 0, 0)),
            pl.BlockSpec((own, width), lambda i: (i, 0)),
            pl.BlockSpec((cols, width), lambda i: (0, 0)),
            pl.BlockSpec((1, 16, width), lambda i: (i, 0, 0)),
        ],
        out_specs=pl.BlockSpec((1, 3 * stat, 128), lambda i: (i, 0, 0)),
        out_shape=jax.ShapeDtypeStruct((n_vocab, 3 * stat, 128), F32),
        scratch_shapes=[pltpu.VMEM((frames, width), F32), pltpu.VMEM((cols + 16, width), BF)],
        cost_estimate=pl.CostEstimate(
            flops=2 * n_vocab * pairs * width * cols,
            bytes_accessed=2 * cols * width,
            transcendentals=n_vocab * pairs * (width + cols),
        ),
    )(enc_all, pred, out_wt, label_w)


def local(
    frames,
    frame_lens,
    labels,
    label_lens,
    phrase_ids,
    phrase_lens,
    phrase_table,
    phrase_w,
    key_w,
    value_w,
    query_w,
    context_w,
    joint_enc_w,
    pred_table,
    pred_w,
    out_w,
):
    n_vocab = lax.axis_size(VOCAB)
    n_phrase = lax.axis_size(PHRASE)
    n_peers = lax.axis_size(PEERS)
    used = frames.shape[0]
    frames_pad = jnp.pad(frames, ((0, PAD - used), (0, 0)))
    queries = mm(frames_pad, query_w).astype(BF)
    asked = lax.all_to_all(
        jnp.broadcast_to(queries[None], (n_peers,) + queries.shape), PEERS, 0, 0, tiled=True
    )

    swap = [(0, 1), (1, 0)]
    slot = jnp.arange(phrase_ids.shape[1], dtype=jnp.int32)
    ids = jnp.where(slot[None, :] < phrase_lens[:, None], phrase_ids, -1)
    keys, values = encode(ids, phrase_table, phrase_w, key_w, value_w)
    other_keys, other_values = lax.ppermute(keys, "c", swap), lax.ppermute(values, "c", swap)

    utts, positions = labels.shape
    frames_dev = used * n_vocab
    tlen = frames_dev * n_phrase // utts
    start = lax.axis_index(PHRASE) * frames_dev
    utt = start // tlen
    own_labels = lax.dynamic_slice_in_dim(labels, utt, 1, 0)[0]
    picked = jnp.concatenate([jnp.zeros((1,), jnp.int32), own_labels[:-1]])
    predictor = mm(pred_table[picked], pred_w).astype(BF).astype(F32)
    vocab_index = lax.axis_index(VOCAB)
    cols = out_w.shape[1]
    out_wt = out_w.T
    column = vocab_index * cols + jnp.arange(cols, dtype=jnp.int32)
    label_w = mm((own_labels[:, None] == column[None, :]).astype(BF), out_wt).astype(BF)

    parts = attend(asked.reshape(n_peers * PAD, -1), keys, values, other_keys, other_values, used)
    parts = lax.all_to_all(parts.reshape(n_peers, PAD, -1), PEERS, 0, 0, tiled=True)
    enc = join(parts, frames_pad, context_w, joint_enc_w, used, n_vocab)
    enc_all = lax.all_to_all(enc, VOCAB, 0, 0, tiled=True)
    stats = joint(enc_all, predictor, out_wt, label_w, used, n_vocab)
    stats = lax.all_to_all(stats, VOCAB, 0, 0, tiled=True)

    own = positions // n_vocab
    pairs = own * frames_dev
    stats = stats.reshape(n_vocab, 3, -1)[:, :, :pairs]
    lse, label, blank = stats[:, 0], stats[:, 1], stats[0, 2]
    peak = jnp.max(lse, 0)
    norm = peak + jnp.log(jnp.sum(jnp.exp(lse - peak), 0))
    label = jnp.sum(label, 0)
    moment = start % tlen + jnp.arange(frames_dev, dtype=jnp.int32)
    position = vocab_index * own + jnp.arange(own, dtype=jnp.int32)
    frame_len = lax.dynamic_slice_in_dim(frame_lens, utt, 1, 0)
    label_len = lax.dynamic_slice_in_dim(label_lens, utt, 1, 0)
    live = (moment < frame_len)[None, :]
    blank = (blank - norm).reshape(own, frames_dev)
    label = (label - norm).reshape(own, frames_dev)
    blank_out = jnp.where(live & (position <= label_len)[:, None], blank, 0.0)
    label_out = jnp.where(live & (position < label_len)[:, None], label, 0.0)
    return (blank_out.T, label_out.T)


def solution(mesh):
    n_phrase, n_vocab = mesh.devices.shape
    fine = Mesh(mesh.devices.reshape(n_phrase // 4, 2, 2, n_vocab // 2, 2), AXES)
    rows = P(AXES, None)
    in_specs = (
        rows,
        P(),
        P(),
        P(),
        rows,
        P(AXES),
        P(),
        P(),
        P(),
        P(),
        P(),
        P(),
        P(),
        P(),
        P(),
        P(None, VOCAB),
    )
    out_specs = (P(PHRASE, VOCAB), P(PHRASE, VOCAB))
    return jax.shard_map(local, mesh=fine, in_specs=in_specs, out_specs=out_specs, check_vma=False)
```

```python
import functools
import math

import jax
import jax.numpy as jnp
from jax import lax
from jax.experimental import pallas as pl
from jax.experimental.pallas import tpu as pltpu
from jax.sharding import Mesh, PartitionSpec as P

HEADS = 4
PAD = 16
AXES = ("y", "zl", "c", "x", "zh")
PHRASE = ("y", "zl", "c")
VOCAB = ("x", "zh")
PEERS = ("y", "zl", "x", "zh")
BF = jnp.bfloat16
F32 = jnp.float32
LOG2E = 1.0 / math.log(2.0)
NT = (((1,), (1,)), ((), ()))


def mm(a, b):
    return jnp.dot(a, b, preferred_element_type=F32)


def encode_kernel(ids_ref, table_ref, phrase_w_ref, key_w_ref, value_w_ref, k_ref, v_ref):
    rows, tokens = ids_ref.shape
    vocab = table_ref.shape[0]
    ids = ids_ref[...]
    lens = jnp.sum(jnp.where(ids >= 0, 1.0, 0.0), 1, keepdims=True)
    lane = lax.broadcasted_iota(jnp.int32, (rows, 128), 1)
    blocks, units = [], []
    for t in range(tokens):
        token = jnp.broadcast_to(ids[:, t : t + 1], (rows, 128))
        blocks.append(lax.shift_right_arithmetic(token, 7).astype(F32).astype(BF))
        units.append(jnp.where((token & 127) == lane, 1.0, 0.0).astype(BF))
    zero = jnp.zeros((rows, 128), BF)
    summed = jnp.zeros((rows, table_ref.shape[1]), F32)
    for pair in range(vocab // 256):
        counts = []
        for block in (2 * pair, 2 * pair + 1):
            count = zero
            for t in range(tokens):
                count += jnp.where(blocks[t] == BF(block), units[t], zero)
            counts.append(count)
        summed += mm(jnp.concatenate(counts, 1), table_ref[pair * 256 : (pair + 1) * 256, :])
    mean = (summed / lens).astype(BF)
    vec = jnp.tanh(mm(mean, phrase_w_ref[...])).astype(BF)
    k_ref[...] = mm(vec, key_w_ref[...]).astype(BF)
    v_ref[...] = mm(vec, value_w_ref[...]).astype(BF)


def encode(ids, table, phrase_w, key_w, value_w):
    phrases, tokens = ids.shape
    vocab, width = table.shape
    tile = 256
    whole = lambda a: pl.BlockSpec(a.shape, lambda i: (0, 0))
    return pl.pallas_call(
        encode_kernel,
        grid=(phrases // tile,),
        in_specs=[
            pl.BlockSpec((tile, tokens), lambda i: (i, 0)),
            whole(table),
            whole(phrase_w),
            whole(key_w),
            whole(value_w),
        ],
        out_specs=[pl.BlockSpec((tile, width), lambda i: (i, 0))] * 2,
        out_shape=[jax.ShapeDtypeStruct((phrases, width), BF)] * 2,
        cost_estimate=pl.CostEstimate(
            flops=40 * phrases * vocab * width,
            bytes_accessed=2 * vocab * width,
            transcendentals=phrases * width,
        ),
    )(ids, table, phrase_w, key_w, value_w)


def attend_kernel(used, scale, q_ref, k0_ref, v0_ref, k1_ref, v1_ref, o_ref):
    rows, tile = q_ref.shape[0], 256
    k = jnp.concatenate([k0_ref[...], k1_ref[...]], 0)
    v = jnp.concatenate([v0_ref[...], v1_ref[...]], 0)
    head = v.shape[1]
    v_ones = jnp.concatenate([v, jnp.ones_like(v)], 1)
    for start in range(0, rows, tile):
        q = q_ref[start : start + tile, :]
        scores = lax.dot_general(q, k, NT, preferred_element_type=F32)
        peak = jnp.max(scores, -1, keepdims=True)
        weights = jnp.exp2((scores - peak) * (scale * LOG2E)).astype(BF)
        sums = mm(weights, v_ones)
        total = sums[:, head:]
        part = sums[:, :head] / total
        rest = peak * scale + jnp.log(total)
        groups = tile // PAD
        shape = (groups, PAD, part.shape[1])
        row = lax.broadcasted_iota(jnp.int32, shape, 1)
        lane = lax.broadcasted_iota(jnp.int32, shape, 2)
        part = part.reshape(shape)
        for piece in range(3):
            sent = rest.astype(BF).astype(F32)
            rest = rest - sent
            line = jnp.sum(jnp.where(lane == row, sent.reshape(shape), 0.0), 1, keepdims=True)
            part = jnp.where(row == used + piece, line, part)
        o_ref[start : start + tile, :] = part.reshape(tile, shape[2]).astype(BF)


def attend(asked, keys, values, other_keys, other_values, used):
    rows, width = asked.shape
    head = width // HEADS
    phrases = keys.shape[0]
    part = pl.BlockSpec((phrases, head), lambda h: (0, h))
    return pl.pallas_call(
        functools.partial(attend_kernel, used, 1.0 / math.sqrt(head)),
        grid=(HEADS,),
        in_specs=[
            pl.BlockSpec((rows, head), lambda h: (0, h)),
            part,
            part,
            part,
            part,
        ],
        out_specs=pl.BlockSpec((rows, head), lambda h: (0, h)),
        out_shape=jax.ShapeDtypeStruct((rows, width), BF),
        cost_estimate=pl.CostEstimate(
            flops=8 * rows * phrases * width,
            bytes_accessed=4 * rows * width + 8 * phrases * width,
            transcendentals=2 * rows * phrases * HEADS,
        ),
    )(asked, keys, values, other_keys, other_values)


def join_kernel(used, parts_ref, frames_ref, context_w_ref, joint_w_ref, o_ref):
    peers, pad, width = parts_ref.shape
    head = width // HEADS
    row = lax.broadcasted_iota(jnp.int32, (peers, pad, head), 1)
    lane = lax.broadcasted_iota(jnp.int32, (peers, pad, head), 2)
    columns = []
    for h in range(HEADS):
        block = parts_ref[:, :, h * head : (h + 1) * head].astype(F32)
        lse = jnp.sum(jnp.where((row >= used) & (row < used + 3), block, 0.0), 1, keepdims=True)
        factor = jnp.exp(lse - jnp.max(lse, 0, keepdims=True))
        factor = factor / jnp.sum(factor, 0, keepdims=True)
        weight = jnp.sum(jnp.where(lane == row, factor, 0.0), -1, keepdims=True)
        columns.append(jnp.sum(weight * block, 0))
    context = jnp.concatenate(columns, 1).astype(BF)
    biased = (frames_ref[...].astype(F32) + mm(context, context_w_ref[...])).astype(BF)
    joint_rows = mm(biased, joint_w_ref[...]).astype(BF)
    for i in range(o_ref.shape[0]):
        o_ref[i] = joint_rows


def join(parts, frames, context_w, joint_w, used, copies):
    parts = pltpu.with_memory_space_constraint(parts, pltpu.VMEM)
    vmem = pl.BlockSpec(memory_space=pltpu.VMEM)
    return pl.pallas_call(
        functools.partial(join_kernel, used),
        in_specs=[vmem] * 4,
        out_specs=vmem,
        out_shape=jax.ShapeDtypeStruct((copies, frames.shape[0], joint_w.shape[1]), BF),
    )(parts, frames, context_w, joint_w)


def joint_kernel(used, enc_ref, pred_ref, out_w_ref, label_w_ref, o_ref, enc_s, w_s):
    groups, pad, width = enc_ref.shape
    frames = groups * used
    own = pred_ref.shape[0]
    cols = out_w_ref.shape[0]
    tile = 256

    @pl.when(pl.program_id(0) == 0)
    def _():
        for g in range(groups):
            enc_s[g * used : (g + 1) * used, :] = enc_ref[g, :used, :].astype(F32)
        w_s[:cols, :] = out_w_ref[...]

    w_s[cols:, :] = label_w_ref[0]
    pred = pred_ref[...]
    stat = o_ref.shape[1] // 3
    for start in range(0, own * frames, tile):
        pieces, at = [], start
        while at < start + tile:
            u, f = at // frames, at % frames
            size = min(frames - f, start + tile - at)
            pieces.append(jnp.tanh(enc_s[f : f + size, :] + pred[u : u + 1, :]).astype(BF))
            at += size
        rows = jnp.concatenate(pieces, 0)
        found = lax.dot_general(w_s[...], rows, NT, preferred_element_type=F32)
        logits = found[:cols]
        peak = jnp.max(logits, 0, keepdims=True)
        total = jnp.sum(jnp.exp2((logits - peak) * LOG2E), 0, keepdims=True)
        lse = peak + jnp.log(total)
        pair = lax.broadcasted_iota(jnp.int32, (own, tile), 1) + start
        low = lax.broadcasted_iota(jnp.int32, (own, tile), 0) * frames
        mine = (pair >= low) & (pair < low + frames)
        label = jnp.sum(jnp.where(mine, found[cols : cols + own], 0.0), 0, keepdims=True)
        for i in range(tile // 128):
            at = start // 128 + i
            piece = slice(i * 128, (i + 1) * 128)
            o_ref[0, at : at + 1, :] = lse[:, piece]
            o_ref[0, stat + at : stat + at + 1, :] = label[:, piece]
            o_ref[0, 2 * stat + at : 2 * stat + at + 1, :] = logits[0:1, piece]


def joint(enc_all, pred, out_wt, label_w, used, n_vocab):
    groups, pad, width = enc_all.shape
    frames = groups * used
    own = pred.shape[0] // n_vocab
    cols = out_wt.shape[0]
    pairs = own * frames
    stat = 8
    enc_all = pltpu.with_memory_space_constraint(enc_all, pltpu.VMEM)
    label_w = jnp.pad(label_w.reshape(n_vocab, own, width), ((0, 0), (0, 16 - own), (0, 0)))
    return pl.pallas_call(
        functools.partial(joint_kernel, used),
        grid=(n_vocab,),
        in_specs=[
            pl.BlockSpec(memory_space=pltpu.VMEM),
            pl.BlockSpec((own, width), lambda i: (i, 0)),
            pl.BlockSpec((cols, width), lambda i: (0, 0)),
            pl.BlockSpec((1, 16, width), lambda i: (i, 0, 0)),
        ],
        out_specs=pl.BlockSpec((1, 3 * stat, 128), lambda i: (i, 0, 0)),
        out_shape=jax.ShapeDtypeStruct((n_vocab, 3 * stat, 128), F32),
        scratch_shapes=[pltpu.VMEM((frames, width), F32), pltpu.VMEM((cols + 16, width), BF)],
        cost_estimate=pl.CostEstimate(
            flops=2 * n_vocab * pairs * width * cols,
            bytes_accessed=2 * cols * width,
            transcendentals=n_vocab * pairs * (width + cols),
        ),
    )(enc_all, pred, out_wt, label_w)


def local(
    frames,
    frame_lens,
    labels,
    label_lens,
    phrase_ids,
    phrase_lens,
    phrase_table,
    phrase_w,
    key_w,
    value_w,
    query_w,
    context_w,
    joint_enc_w,
    pred_table,
    pred_w,
    out_w,
):
    n_vocab = lax.axis_size(VOCAB)
    n_phrase = lax.axis_size(PHRASE)
    n_peers = lax.axis_size(PEERS)
    used = frames.shape[0]
    frames_pad = jnp.pad(frames, ((0, PAD - used), (0, 0)))
    queries = mm(frames_pad, query_w).astype(BF)
    asked = lax.all_to_all(
        jnp.broadcast_to(queries[None], (n_peers,) + queries.shape), PEERS, 0, 0, tiled=True
    )

    swap = [(0, 1), (1, 0)]
    slot = jnp.arange(phrase_ids.shape[1], dtype=jnp.int32)
    ids = jnp.where(slot[None, :] < phrase_lens[:, None], phrase_ids, -1)
    keys, values = encode(ids, phrase_table, phrase_w, key_w, value_w)
    other_keys, other_values = lax.ppermute(keys, "c", swap), lax.ppermute(values, "c", swap)

    utts, positions = labels.shape
    frames_dev = used * n_vocab
    tlen = frames_dev * n_phrase // utts
    start = lax.axis_index(PHRASE) * frames_dev
    utt = start // tlen
    own_labels = lax.dynamic_slice_in_dim(labels, utt, 1, 0)[0]
    picked = jnp.concatenate([jnp.zeros((1,), jnp.int32), own_labels[:-1]])
    predictor = mm(pred_table[picked], pred_w).astype(BF).astype(F32)
    vocab_index = lax.axis_index(VOCAB)
    cols = out_w.shape[1]
    out_wt = out_w.T
    column = vocab_index * cols + jnp.arange(cols, dtype=jnp.int32)
    label_w = mm((own_labels[:, None] == column[None, :]).astype(BF), out_wt).astype(BF)

    parts = attend(asked.reshape(n_peers * PAD, -1), keys, values, other_keys, other_values, used)
    parts = lax.all_to_all(parts.reshape(n_peers, PAD, -1), PEERS, 0, 0, tiled=True)
    enc = join(parts, frames_pad, context_w, joint_enc_w, used, n_vocab)
    enc_all = lax.all_to_all(enc, VOCAB, 0, 0, tiled=True)
    stats = joint(enc_all, predictor, out_wt, label_w, used, n_vocab)
    stats = lax.all_to_all(stats, VOCAB, 0, 0, tiled=True)

    own = positions // n_vocab
    pairs = own * frames_dev
    stats = stats.reshape(n_vocab, 3, -1)[:, :, :pairs]
    lse, label, blank = stats[:, 0], stats[:, 1], stats[0, 2]
    peak = jnp.max(lse, 0)
    norm = peak + jnp.log(jnp.sum(jnp.exp(lse - peak), 0))
    label = jnp.sum(label, 0)
    moment = start % tlen + jnp.arange(frames_dev, dtype=jnp.int32)
    position = vocab_index * own + jnp.arange(own, dtype=jnp.int32)
    frame_len = lax.dynamic_slice_in_dim(frame_lens, utt, 1, 0)
    label_len = lax.dynamic_slice_in_dim(label_lens, utt, 1, 0)
    live = (moment < frame_len)[None, :]
    blank = (blank - norm).reshape(own, frames_dev)
    label = (label - norm).reshape(own, frames_dev)
    blank_out = jnp.where(live & (position <= label_len)[:, None], blank, 0.0)
    label_out = jnp.where(live & (position < label_len)[:, None], label, 0.0)
    return (blank_out.T, label_out.T)


def solution(mesh):
    n_phrase, n_vocab = mesh.devices.shape
    fine = Mesh(mesh.devices.reshape(n_phrase // 4, 2, 2, n_vocab // 2, 2), AXES)
    rows = P(AXES, None)
    in_specs = (
        rows,
        P(),
        P(),
        P(),
        rows,
        P(AXES),
        P(),
        P(),
        P(),
        P(),
        P(),
        P(),
        P(),
        P(),
        P(),
        P(None, VOCAB),
    )
    out_specs = (P(PHRASE, VOCAB), P(PHRASE, VOCAB))
    return jax.shard_map(local, mesh=fine, in_specs=in_specs, out_specs=out_specs, check_vma=False)
```
